32 devices in a mesh: ka: 8 (over z, x), ga: 4 (over y, core).
Axes of the slice: x: 2, y: 2, z: 4, core: 2. Of those that a mesh axis runs over, the one named last changes fastest.
Arguments:
- coefficients: bfloat16 [8, 2, 256, 55296], P('ka', None, 'ga'), may hold values from -0.4375 to 0.4375
- shift_map: int32 [8, 3, 55296], P('ka', None, 'ga'), may hold values from 0 to 55295, as said below
- phase_angle: float32 [8, 3], P('ka'), may hold values from -3.140625 to 3.140625
Outputs:
- intersections: float32 [8, 3, 2, 256, 256], P('ka', None, None, 'ga')
The draws below stay inside these ranges and needn't reach their ends.
Inputs may be any that keep to these rules, and one draw needn't show every extreme that they name: Each aligned block of 13824 consecutive entries of shift_map[k, b] is a permutation of the indices of that same block; it maps aligned tiles of 128 entries onto aligned tiles of 128 indices.
All inputs are finite; a program needn't handle non-finite values.
Results may differ from the reference program's by a relative error of at most 0.0003.
Values may be sent and summed in bfloat16 or wider, within the bound.
A program may use at most 192 MiB of HBM per device.

```python
import jax
import jax.numpy as jnp
from jax import lax

BANDS = 256
NPW = 55296
KPOINTS = 8
G_DEV = 13824


def draw_shift_map(key, part):
    tiles = G_DEV // 128
    shards = NPW // G_DEV
    count = KPOINTS * 3 * shards
    first_key = jax.random.fold_in(key, 11)
    second_key = jax.random.fold_in(key, 23)
    tile_order = jax.vmap(lambda sub: jax.random.permutation(sub, tiles))(jax.random.split(first_key, count))
    inner = jax.vmap(lambda sub: jax.random.permutation(sub, 128))(jax.random.split(second_key, count * tiles))
    inner = inner.reshape(count, tiles, 128)
    local = tile_order[:, :, None] * 128 + inner
    base = jnp.arange(count, dtype=jnp.int32) % shards * G_DEV
    full = local.reshape(count, G_DEV) + base[:, None]
    return full.reshape(KPOINTS, 3, NPW).astype(jnp.int32)


def level_of(key, shape, cuts, least, top_value):
    level = 1.0
    for dim, blocks in cuts:
        heights = jax.random.uniform(jax.random.fold_in(jax.random.fold_in(key, 6), dim), (blocks,), jnp.float32, least / len(cuts), top_value / len(cuts))
        level = level * jnp.repeat(jnp.exp(heights), shape[dim] // blocks).reshape((-1,) + (1,) * (len(shape) - 1 - dim))
    return level


def bell_draw(own_key, extent, deviation, reach, pieces=(), kind=jnp.bfloat16):
    level = level_of(own_key, extent, pieces, -0.22, 0.18) if pieces else 1.0
    drawn = jax.random.normal(own_key, extent, jnp.float32) * deviation * level
    return jnp.minimum(jnp.maximum(drawn, -reach), reach).astype(kind)


def setup_inputs(seed: int = 0) -> dict:
    key_list = jax.random.split(jax.random.key(seed), 4)
    return {
        "coefficients": bell_draw(key_list[0], (KPOINTS, 2, BANDS, NPW), 0.07, 0.4375, ((0, 8), (2, 4))),
        "shift_map": draw_shift_map(jax.random.fold_in(key_list[3], 71), 0),
        "phase_angle": jnp.clip(jax.random.uniform(key_list[2], (KPOINTS, 3), jnp.float32, -3.140625, 3.140625), -3.140625, 3.140625),
    }


def reference(coefficients, shift_map, phase_angle):
    def one_point(kk):
        own = coefficients[kk]
        left = jnp.concatenate([own[0], own[1]], axis=1)
        nbrs = ((kk + 4) % KPOINTS, jnp.bitwise_xor(kk, 2), jnp.bitwise_xor(kk, 1))
        blocks = []
        for direction in range(3):
            other = coefficients[nbrs[direction].astype(jnp.int32)]
            moved = jnp.take(other, shift_map[kk, direction], axis=2)
            right_re = jnp.concatenate([moved[0], moved[1]], axis=1)
            right_im = jnp.concatenate([moved[1], -moved[0]], axis=1)
            real_part = lax.dot_general(left, right_re, (((1,), (1,)), ((), ())), preferred_element_type=jnp.float32)
            imag_part = lax.dot_general(left, right_im, (((1,), (1,)), ((), ())), preferred_element_type=jnp.float32)
            cosine = jnp.cos(phase_angle[kk, direction])
            sine = jnp.sin(phase_angle[kk, direction])
            blocks.append(jnp.stack([cosine * real_part - sine * imag_part, sine * real_part + cosine * imag_part]))
        return jnp.stack(blocks)

    return lax.map(one_point, jnp.arange(KPOINTS, dtype=jnp.int32))
```

```python
import functools

import jax
import jax.numpy as jnp
from jax import lax
from jax.experimental import pallas as pl
from jax.experimental.pallas import tpu as pltpu
from jax.sharding import PartitionSpec as P

LANES = 128
F32 = jnp.float32
NT = (((1,), (1,)), ((), ()))


def passed_along(value, axis, steps):
    count = lax.axis_size(axis)
    pairs = [(source, (source + steps) % count) for source in range(count)]
    return lax.ppermute(value, axis, pairs)


def swapped(block, axis, bit):
    count = lax.axis_size(axis)
    route = []
    for low in range(count):
        high = low | 1 << bit
        if high != low and high < count:
            route += [(low, high), (high, low)]
    return lax.ppermute(block, axis, route)


def cross_terms(left, moved):
    prods = jnp.einsum("amg,bng->abmn", left, moved, preferred_element_type=jnp.float32)
    real_part = prods[0, 0] + prods[1, 1]
    imag_part = prods[0, 1] - prods[1, 0]
    return jnp.stack([real_part, imag_part])


def rotated_by(phase, real_part, imag_part):
    cosine = jnp.cos(phase)[:, None, None]
    sine = jnp.sin(phase)[:, None, None]
    return jnp.stack(
        [cosine * real_part - sine * imag_part, sine * real_part + cosine * imag_part], axis=1
    )


def general(coefficients, shift_map, phase_angle):
    own = lax.all_to_all(coefficients, "ga", split_axis=3, concat_axis=2, tiled=True)
    next_x = passed_along(own, "ka", -4)
    next_y = swapped(own, "ka", 1)
    next_z = swapped(own, "ka", 0)
    block_width = own.shape[3]
    local_map = shift_map[0] - lax.axis_index("ga") * block_width
    left = own[0]
    movers = []
    for direction, other in enumerate((next_x, next_y, next_z)):
        movers.append(jnp.take(other[0], local_map[direction], axis=2))
    parts = jnp.stack([cross_terms(left, moved) for moved in movers])
    summed = lax.psum_scatter(
        jnp.transpose(parts, (2, 0, 1, 3)), "ga", scatter_dimension=0, tiled=True
    )
    summed = jnp.transpose(summed, (1, 2, 0, 3))
    return rotated_by(phase_angle[0], summed[:, 0], summed[:, 1])[None]


def largest_divisor(count, most):
    return max(d for d in range(1, most + 1) if count % d == 0)


def copy_body(index, source, target):
    target[...] = source[...]


def block_of(source, index, width):
    parts, rows, _ = source.shape
    per = largest_divisor(width // LANES, 36)
    cols, steps = per * LANES, width // (per * LANES)
    grid_spec = pltpu.PrefetchScalarGridSpec(
        num_scalar_prefetch=1,
        grid=(steps,),
        in_specs=[pl.BlockSpec((parts, rows, cols), lambda i, at: (0, 0, at[0] * steps + i))],
        out_specs=pl.BlockSpec((parts, rows, cols), lambda i, at: (0, 0, i)),
    )
    return pl.pallas_call(
        copy_body,
        grid_spec=grid_spec,
        out_shape=jax.ShapeDtypeStruct((parts, rows, width), source.dtype),
        cost_estimate=pl.CostEstimate(flops=0, bytes_accessed=4 * parts * rows * width, transcendentals=0),
    )(index.reshape(1), source)


def pair_body(unroll, tile1, tile2, *refs):
    pieces = refs[:4]
    b_ref, rows1, rows2, near_ref, far_ref, acc = refs[4:]
    step = pl.program_id(0)
    iota = lax.broadcasted_iota(jnp.int32, (LANES, LANES), 0)
    columns = []
    for i in range(unroll):
        t = step * unroll + i
        s1, s2 = tile1[t], tile2[t]
        pick1 = jnp.where(iota == rows1[pl.ds(t, 1), :], 1.0, 0.0).astype(jnp.bfloat16)
        pick2 = jnp.where(iota == rows2[pl.ds(s2, 1), :], 1.0, 0.0).astype(jnp.bfloat16)
        b1 = b_ref[:, pl.ds(pl.multiple_of(s1 * LANES, LANES), LANES)]
        b2 = b_ref[:, pl.ds(pl.multiple_of(s2 * LANES, LANES), LANES)]
        g1 = jnp.dot(b1, pick1, preferred_element_type=F32).astype(jnp.bfloat16)
        g2 = lax.dot_general(b2, pick2, NT, preferred_element_type=F32).astype(jnp.bfloat16)
        columns.append(jnp.concatenate([g1, g2], axis=0))
    right = jnp.concatenate(columns, axis=1)
    left = jnp.concatenate([piece[...] for piece in pieces], axis=0)
    term = lax.dot_general(left, right, NT, preferred_element_type=F32)

    @pl.when(step == 0)
    def _():
        acc[...] = term

    @pl.when(step > 0)
    def _():
        acc[...] += term

    @pl.when(step == pl.num_programs(0) - 1)
    def _():
        nb = b_ref.shape[0] // 2
        mb = pieces[0].shape[0] // 2
        for r in range(4):
            re = acc[2 * r * mb : (2 * r + 1) * mb, :]
            im = acc[(2 * r + 1) * mb : (2 * r + 2) * mb, :]
            near_ref[0, r] = re[:, :nb] + im[:, nb : 2 * nb]
            near_ref[1, r] = re[:, nb : 2 * nb] - im[:, :nb]
            far_ref[0, r] = (re[:, 2 * nb : 3 * nb] + im[:, 3 * nb :]).T
            far_ref[1, r] = (im[:, 2 * nb : 3 * nb] - re[:, 3 * nb :]).T


def pair_products(pieces, other, tile1, tile2, rows1, rows2):
    _, mb, width = pieces[0].shape
    nb = other.shape[1]
    tiles = width // LANES
    unroll = largest_divisor(tiles, 6)
    flat = [piece.reshape(2 * mb, width) for piece in pieces]
    whole = lambda shape: pl.BlockSpec(shape, lambda i, *_: (0,) * len(shape))
    grid_spec = pltpu.PrefetchScalarGridSpec(
        num_scalar_prefetch=2,
        grid=(tiles // unroll,),
        in_specs=[pl.BlockSpec((2 * mb, unroll * LANES), lambda i, *_: (0, i))] * 4
        + [whole((2 * nb, width)), whole((tiles, LANES)), whole((tiles, LANES))],
        out_specs=[whole((2, 4, mb, nb)), whole((2, 4, nb, mb))],
        scratch_shapes=[pltpu.VMEM((8 * mb, 4 * nb), F32)],
    )
    return pl.pallas_call(
        functools.partial(pair_body, unroll),
        grid_spec=grid_spec,
        out_shape=[
            jax.ShapeDtypeStruct((2, 4, mb, nb), F32),
            jax.ShapeDtypeStruct((2, 4, nb, mb), F32),
        ],
        cost_estimate=pl.CostEstimate(
            flops=64 * mb * nb * width, bytes_accessed=(16 * mb + 4 * nb) * width, transcendentals=0
        ),
    )(tile1, tile2, *flat, other.reshape(2 * nb, width), rows1, rows2)


def paired(coefficients, shift_map, phase_angle):
    raw = coefficients[0]
    k = lax.axis_index("ka")
    j = lax.axis_index("ga")
    half = lax.axis_size("ga") // 2
    width = shift_map.shape[2]
    tiles = width // LANES
    parity = (k ^ (k >> 1) ^ (k >> 2)) & 1
    mine = parity * half + j // 2
    theirs = (1 - parity) * half + j // 2
    mates = lambda value, mask: lax.ppermute(
        value, "ga", [(s, s ^ mask) for s in range(lax.axis_size("ga"))]
    )
    flips = (4, 2, 1)
    hop = lambda value, b: lax.ppermute(
        value, "ka", [(s, s ^ flips[b]) for s in range(lax.axis_size("ka"))]
    )

    out_relay = block_of(raw, theirs ^ 1, width)
    out_own = block_of(raw, theirs, width)
    relay = mates(out_relay, 2)
    first = [hop(out_own, b) for b in range(3)]
    piece0 = block_of(raw, mine, width)
    piece1 = mates(piece0, 1)
    second = [hop(relay, b) for b in range(3)]
    give = block_of(raw, mine ^ 1, width)
    give, relay = lax.optimization_barrier((give, relay))
    piece2 = mates(give, 2)
    piece3 = mates(piece2, 1)
    pieces = [piece0, piece1, piece2, piece3]

    maps = shift_map[0]
    blocks = jnp.stack([maps] + [mates(maps, r) for r in (1, 2, 3)])
    mine_map = lax.dynamic_index_in_dim(blocks, mine ^ j, 0, keepdims=False) - mine * width
    give_map = lax.dynamic_index_in_dim(blocks, theirs ^ j, 0, keepdims=False) - theirs * width
    tables = []
    place = jnp.arange(tiles, dtype=jnp.int32)
    for b in range(3):
        to_other = mine_map[b].reshape(tiles, LANES)
        to_mine = hop(give_map[b], b).reshape(tiles, LANES)
        tile1 = to_other[:, 0] // LANES
        tile_of = to_mine[:, 0] // LANES
        tile2 = jnp.sum(jnp.where(tile_of[None, :] == place[:, None], place[None, :], 0), axis=1)
        tables.append((tile1, tile2, to_other % LANES, to_mine % LANES))

    results = [None] * 3
    for b in (2, 1, 0):
        near0, far0 = pair_products(pieces, first[b], *tables[b])
        near1, far1 = pair_products(pieces, second[b], *tables[b])
        came = mates(far1, 2)
        back = far0 + jnp.stack([came[:, r ^ 2] for r in range(4)], axis=1)
        total = hop(back, b)
        near = jnp.stack([near0, near1], axis=1)
        got = [near[:, :, 0]] + [mates(near[:, :, r], r) for r in (1, 2, 3)]
        blocks_n = [total[:, t] + got[t][:, 0] + got[t ^ 2][:, 1] for t in range(4)]
        results[b] = jnp.stack(blocks_n)
    stacked = jnp.stack(results, axis=1)
    ordered = [lax.dynamic_index_in_dim(stacked, j ^ q, 0, keepdims=False) for q in range(4)]
    summed = jnp.concatenate(ordered, axis=-1)
    return rotated_by(phase_angle[0], summed[:, 0], summed[:, 1])[None]


def solution(mesh):
    in_specs = (P("ka", None, "ga", None), P("ka", None, "ga"), P("ka", None))
    out_specs = P("ka", None, None, "ga", None)
    both_ways = mesh.shape["ka"] == 8 and mesh.shape["ga"] == 4
    local = paired if both_ways else general
    return jax.shard_map(local, mesh=mesh, in_specs=in_specs, out_specs=out_specs, check_vma=False)
```

```python
import functools

import jax
import jax.numpy as jnp
from jax import lax
from jax.experimental import pallas as pl
from jax.experimental.pallas import tpu as pltpu
from jax.sharding import PartitionSpec as P


LANES = 128
UNROLL = 6
F32 = jnp.float32
NT = (((1,), (1,)), ((), ()))


def passed_along(value, axis, steps):
    count = lax.axis_size(axis)
    pairs = [(source, (source + steps) % count) for source in range(count)]
    return lax.ppermute(value, axis, pairs)


def swapped(block, axis, bit):
    count = lax.axis_size(axis)
    route = []
    for low in range(count):
        high = low | 1 << bit
        if high != low and high < count:
            route += [(low, high), (high, low)]
    return lax.ppermute(block, axis, route)


def cross_terms(left, moved):
    prods = jnp.einsum("amg,bng->abmn", left, moved, preferred_element_type=jnp.float32)
    real_part = prods[0, 0] + prods[1, 1]
    imag_part = prods[0, 1] - prods[1, 0]
    return jnp.stack([real_part, imag_part])


def rotated_by(phase, real_part, imag_part):
    cosine = jnp.cos(phase)[:, None, None]
    sine = jnp.sin(phase)[:, None, None]
    return jnp.stack(
        [cosine * real_part - sine * imag_part, sine * real_part + cosine * imag_part], axis=1
    )


def general(coefficients, shift_map, phase_angle):
    own = lax.all_to_all(coefficients, "ga", split_axis=3, concat_axis=2, tiled=True)
    next_x = passed_along(own, "ka", -4)
    next_y = swapped(own, "ka", 1)
    next_z = swapped(own, "ka", 0)
    block_width = own.shape[3]
    local_map = shift_map[0] - lax.axis_index("ga") * block_width
    left = own[0]
    movers = []
    for direction, other in enumerate((next_x, next_y, next_z)):
        movers.append(jnp.take(other[0], local_map[direction], axis=2))
    parts = jnp.stack([cross_terms(left, moved) for moved in movers])
    summed = lax.psum_scatter(
        jnp.transpose(parts, (2, 0, 1, 3)), "ga", scatter_dimension=0, tiled=True
    )
    summed = jnp.transpose(summed, (1, 2, 0, 3))
    return rotated_by(phase_angle[0], summed[:, 0], summed[:, 1])[None]


def largest_divisor(count, most):
    return max(d for d in range(1, most + 1) if count % d == 0)


def copy_body(index, source, target):
    target[...] = source[...]


def block_of(source, index, width):
    parts, rows, _ = source.shape
    per = largest_divisor(width // LANES, 36)
    cols, steps = per * LANES, width // (per * LANES)
    grid_spec = pltpu.PrefetchScalarGridSpec(
        num_scalar_prefetch=1,
        grid=(steps,),
        in_specs=[pl.BlockSpec((parts, rows, cols), lambda i, at: (0, 0, at[0] * steps + i))],
        out_specs=pl.BlockSpec((parts, rows, cols), lambda i, at: (0, 0, i)),
    )
    return pl.pallas_call(
        copy_body,
        grid_spec=grid_spec,
        out_shape=jax.ShapeDtypeStruct((parts, rows, width), source.dtype),
        cost_estimate=pl.CostEstimate(flops=0, bytes_accessed=4 * parts * rows * width, transcendentals=0),
    )(index.reshape(1), source)


def pair_body(unroll, tile1, tile2, *refs):
    pieces = refs[:4]
    others = refs[4:-5]
    rows1, rows2, near_ref, far_ref, acc = refs[-5:]
    step = pl.program_id(0)
    iota = lax.broadcasted_iota(jnp.int32, (LANES, LANES), 0)

    def tile_of(s):
        at = pl.ds(pl.multiple_of(s * LANES, LANES), LANES)
        value = others[0][:, at]
        for other in others[1:]:
            value = value + other[:, at]
        return value

    columns = []
    for i in range(unroll):
        t = step * unroll + i
        s1, s2 = tile1[t], tile2[t]
        pick1 = jnp.where(iota == rows1[pl.ds(t, 1), :], 1.0, 0.0).astype(jnp.bfloat16)
        pick2 = jnp.where(iota == rows2[pl.ds(s2, 1), :], 1.0, 0.0).astype(jnp.bfloat16)
        g1 = jnp.dot(tile_of(s1), pick1, preferred_element_type=F32).astype(jnp.bfloat16)
        g2 = lax.dot_general(tile_of(s2), pick2, NT, preferred_element_type=F32).astype(jnp.bfloat16)
        columns.append(jnp.concatenate([g1, g2], axis=0))
    right = jnp.concatenate(columns, axis=1)
    left = jnp.concatenate([piece[...] for piece in pieces], axis=0)
    term = lax.dot_general(left, right, NT, preferred_element_type=F32)

    @pl.when(step == 0)
    def _():
        acc[...] = term

    @pl.when(step > 0)
    def _():
        acc[...] += term

    @pl.when(step == pl.num_programs(0) - 1)
    def _():
        nb = others[0].shape[0] // 2
        mb = pieces[0].shape[0] // 2
        for r in range(4):
            re = acc[2 * r * mb : (2 * r + 1) * mb, :]
            im = acc[(2 * r + 1) * mb : (2 * r + 2) * mb, :]
            near_ref[r, 0] = re[:, :nb] + im[:, nb : 2 * nb]
            near_ref[r, 1] = re[:, nb : 2 * nb] - im[:, :nb]
            far_ref[r, 0] = (re[:, 2 * nb : 3 * nb] + im[:, 3 * nb :]).T
            far_ref[r, 1] = (im[:, 2 * nb : 3 * nb] - re[:, 3 * nb :]).T


def pair_products(pieces, others, tile1, tile2, rows1, rows2):
    _, mb, width = pieces[0].shape
    nb = others[0].shape[1]
    tiles = width // LANES
    unroll = largest_divisor(tiles, UNROLL)
    flat = [piece.reshape(2 * mb, width) for piece in pieces]
    flat_others = [other.reshape(2 * nb, width) for other in others]
    whole = lambda shape: pl.BlockSpec(shape, lambda i, *_: (0,) * len(shape))
    grid_spec = pltpu.PrefetchScalarGridSpec(
        num_scalar_prefetch=2,
        grid=(tiles // unroll,),
        in_specs=[pl.BlockSpec((2 * mb, unroll * LANES), lambda i, *_: (0, i))] * 4
        + [whole((2 * nb, width))] * len(others)
        + [whole((tiles, LANES)), whole((tiles, LANES))],
        out_specs=[whole((4, 2, mb, nb)), whole((4, 2, nb, mb))],
        scratch_shapes=[pltpu.VMEM((8 * mb, 4 * nb), F32)],
    )
    return pl.pallas_call(
        functools.partial(pair_body, unroll),
        grid_spec=grid_spec,
        out_shape=[
            jax.ShapeDtypeStruct((4, 2, mb, nb), F32),
            jax.ShapeDtypeStruct((4, 2, nb, mb), F32),
        ],
        cost_estimate=pl.CostEstimate(
            flops=160 * mb * nb * width, bytes_accessed=(16 * mb + 4 * nb) * width, transcendentals=0
        ),
    )(tile1, tile2, *flat, *flat_others, rows1, rows2)


def paired(coefficients, shift_map, phase_angle):
    return paired_points(coefficients, shift_map, phase_angle)


def paired_points(coefficients, shift_map, phase_angle):
    raw = coefficients[0]
    k = lax.axis_index("ka")
    j = lax.axis_index("ga")
    points, group = lax.axis_size("ka"), lax.axis_size("ga")
    half = group // 2
    width = shift_map.shape[2]
    tiles = width // LANES
    parity_of = lambda point: (point ^ (point >> 1) ^ (point >> 2)) & 1
    parity = parity_of(k)
    mine = parity * half + j // 2
    theirs = (1 - parity) * half + j // 2
    flips = (4, 2, 1)
    mates = lambda value, mask: lax.ppermute(value, "ga", [(s, s ^ mask) for s in range(group)])
    both = lambda value, pairs: lax.ppermute(value, ("ka", "ga"), pairs)
    middle = [(s, s ^ 6) for s in range(points) if (s >> 1) in (1, 2)]
    outward = [(s, s ^ 2) for s in range(points) if (s >> 1) in (1, 2)]
    hop = lambda value, b: lax.ppermute(value, "ka", [(s, s ^ flips[b]) for s in range(points)])
    along = lambda value, pairs: lax.ppermute(value, "ka", pairs)

    maps = shift_map[0]
    arrived = [
        both(
            value,
            [
                ((p ^ flip) * group + parity_of(p) * half + y, p * group + 2 * y)
                for p in range(points)
                for y in range(half)
            ],
        )
        for value, flip in [(maps, 0)] + [(maps[b : b + 1], flips[b]) for b in range(3)]
    ]
    out_own = block_of(raw, theirs, width)
    out_own, *arrived = lax.optimization_barrier((out_own, *arrived))
    arrived = jnp.concatenate(arrived, axis=0)
    arrived = jnp.where(j % 2 == 0, arrived, mates(arrived, 1)) - mine * width

    first1 = hop(out_own, 1)
    parked0 = along(out_own, middle)
    relay_at, out_own = lax.optimization_barrier((theirs ^ 1, out_own))
    out_relay = block_of(raw, relay_at, width)
    relay = mates(out_relay, 2)
    first2 = hop(out_own, 2)
    piece0 = block_of(raw, mine, width)
    piece1 = mates(piece0, 1)
    first0 = [along(first1, middle)]
    first0 += [along(parked0, outward)]
    second1 = hop(relay, 1)
    parked1 = along(relay, middle)
    second2 = hop(relay, 2)
    give = block_of(raw, mine ^ 1, width)
    give, relay = lax.optimization_barrier((give, relay))
    piece2 = mates(give, 2)
    piece3 = mates(piece2, 1)
    pieces = [piece0, piece1, piece2, piece3]
    second0 = [along(second1, middle)]
    second0 += [along(parked1, outward)]
    early = [first0, [first1], [first2]]
    late = [second0, [second1], [second2]]

    tables = []
    place = jnp.arange(tiles, dtype=jnp.int32)
    for b in range(3):
        to_other = arrived[b].reshape(tiles, LANES)
        to_mine = arrived[3 + b].reshape(tiles, LANES)
        tile1 = to_other[:, 0] // LANES
        tile_of = to_mine[:, 0] // LANES
        tile2 = jnp.sum(jnp.where(tile_of[None, :] == place[:, None], place[None, :], 0), axis=1)
        tables.append((tile1, tile2, to_other % LANES, to_mine % LANES))

    sums = [None] * 3
    for b, which in ((2, 0), (2, 1), (1, 0), (1, 1), (0, 0), (0, 1)):
        near, far = pair_products(pieces, (early, late)[which][b], *tables[b])
        mask = 2 * which
        far = both(
            far,
            [
                (p * group + s, (p ^ flips[b]) * group + (s ^ mask))
                for p in range(points)
                for s in range(group)
            ],
        )
        got = [near[0]] + [mates(near[r], r) for r in (1, 2, 3)]
        term = [far[t ^ mask] + got[t ^ mask] for t in range(4)]
        sums[b] = term if sums[b] is None else [x + y for x, y in zip(sums[b], term)]
    stacked = jnp.stack([jnp.stack(one) for one in sums], axis=1)
    ordered = [lax.dynamic_index_in_dim(stacked, j ^ q, 0, keepdims=False) for q in range(4)]
    summed = jnp.concatenate(ordered, axis=-1)
    return rotated_by(phase_angle[0], summed[:, 0], summed[:, 1])[None]


def solution(mesh):
    in_specs = (P("ka", None, "ga", None), P("ka", None, "ga"), P("ka", None))
    out_specs = P("ka", None, None, "ga", None)
    both_ways = mesh.shape["ka"] == 8 and mesh.shape["ga"] == 4
    local = paired if both_ways else general
    return jax.shard_map(local, mesh=mesh, in_specs=in_specs, out_specs=out_specs, check_vma=False)
```

```python
import functools

import jax
import jax.numpy as jnp
from jax import lax
from jax.experimental import pallas as pl
from jax.experimental.pallas import tpu as pltpu
from jax.sharding import PartitionSpec as P


LANES = 128
UNROLL = 27
F32 = jnp.float32
NT = (((1,), (1,)), ((), ()))


def passed_along(value, axis, steps):
    count = lax.axis_size(axis)
    pairs = [(source, (source + steps) % count) for source in range(count)]
    return lax.ppermute(value, axis, pairs)


def swapped(block, axis, bit):
    count = lax.axis_size(axis)
    route = []
    for low in range(count):
        high = low | 1 << bit
        if high != low and high < count:
            route += [(low, high), (high, low)]
    return lax.ppermute(block, axis, route)


def cross_terms(left, moved):
    prods = jnp.einsum("amg,bng->abmn", left, moved, preferred_element_type=jnp.float32)
    real_part = prods[0, 0] + prods[1, 1]
    imag_part = prods[0, 1] - prods[1, 0]
    return jnp.stack([real_part, imag_part])


def rotated_by(phase, real_part, imag_part):
    cosine = jnp.cos(phase)[:, None, None]
    sine = jnp.sin(phase)[:, None, None]
    return jnp.stack(
        [cosine * real_part - sine * imag_part, sine * real_part + cosine * imag_part], axis=1
    )


def general(coefficients, shift_map, phase_angle):
    own = lax.all_to_all(coefficients, "ga", split_axis=3, concat_axis=2, tiled=True)
    next_x = passed_along(own, "ka", -4)
    next_y = swapped(own, "ka", 1)
    next_z = swapped(own, "ka", 0)
    block_width = own.shape[3]
    local_map = shift_map[0] - lax.axis_index("ga") * block_width
    left = own[0]
    movers = []
    for direction, other in enumerate((next_x, next_y, next_z)):
        movers.append(jnp.take(other[0], local_map[direction], axis=2))
    parts = jnp.stack([cross_terms(left, moved) for moved in movers])
    summed = lax.psum_scatter(
        jnp.transpose(parts, (2, 0, 1, 3)), "ga", scatter_dimension=0, tiled=True
    )
    summed = jnp.transpose(summed, (1, 2, 0, 3))
    return rotated_by(phase_angle[0], summed[:, 0], summed[:, 1])[None]


def largest_divisor(count, most):
    return max(d for d in range(1, most + 1) if count % d == 0)


def copy_body(index, source, target):
    target[...] = source[...]


def block_of(source, index, width):
    parts, rows, _ = source.shape
    per = largest_divisor(width // LANES, 36)
    cols, steps = per * LANES, width // (per * LANES)
    grid_spec = pltpu.PrefetchScalarGridSpec(
        num_scalar_prefetch=1,
        grid=(steps,),
        in_specs=[pl.BlockSpec((parts, rows, cols), lambda i, at: (0, 0, at[0] * steps + i))],
        out_specs=pl.BlockSpec((parts, rows, cols), lambda i, at: (0, 0, i)),
    )
    return pl.pallas_call(
        copy_body,
        grid_spec=grid_spec,
        out_shape=jax.ShapeDtypeStruct((parts, rows, width), source.dtype),
        cost_estimate=pl.CostEstimate(flops=0, bytes_accessed=4 * parts * rows * width, transcendentals=0),
    )(index.reshape(1), source)


def pair_body(unroll, tile1, tile2, *refs):
    pieces = refs[:4]
    others = refs[4:-5]
    rows1, rows2, near_ref, far_ref, acc = refs[-5:]
    step = pl.program_id(0)
    iota = lax.broadcasted_iota(jnp.int32, (LANES, LANES), 0)

    def tile_of(s):
        at = pl.ds(pl.multiple_of(s * LANES, LANES), LANES)
        value = others[0][:, at]
        for other in others[1:]:
            value = value + other[:, at]
        return value

    columns = []
    for i in range(unroll):
        t = step * unroll + i
        s1, s2 = tile1[t], tile2[t]
        pick1 = jnp.where(iota == rows1[pl.ds(t, 1), :], 1.0, 0.0).astype(jnp.bfloat16)
        pick2 = jnp.where(iota == rows2[pl.ds(s2, 1), :], 1.0, 0.0).astype(jnp.bfloat16)
        g1 = jnp.dot(tile_of(s1), pick1, preferred_element_type=F32).astype(jnp.bfloat16)
        g2 = lax.dot_general(tile_of(s2), pick2, NT, preferred_element_type=F32).astype(jnp.bfloat16)
        columns.append(jnp.concatenate([g1, g2], axis=0))
    right = jnp.concatenate(columns, axis=1)
    left = jnp.concatenate([piece[...] for piece in pieces], axis=0)
    term = lax.dot_general(left, right, NT, preferred_element_type=F32)

    @pl.when(step == 0)
    def _():
        acc[...] = term

    @pl.when(step > 0)
    def _():
        acc[...] += term

    @pl.when(step == pl.num_programs(0) - 1)
    def _():
        nb = others[0].shape[0] // 2
        mb = pieces[0].shape[0] // 2
        for r in range(4):
            re = acc[2 * r * mb : (2 * r + 1) * mb, :]
            im = acc[(2 * r + 1) * mb : (2 * r + 2) * mb, :]
            near_ref[r, 0] = re[:, :nb] + im[:, nb : 2 * nb]
            near_ref[r, 1] = re[:, nb : 2 * nb] - im[:, :nb]
            far_ref[r, 0] = (re[:, 2 * nb : 3 * nb] + im[:, 3 * nb :]).T
            far_ref[r, 1] = (im[:, 2 * nb : 3 * nb] - re[:, 3 * nb :]).T


def pair_products(pieces, others, tile1, tile2, rows1, rows2):
    _, mb, width = pieces[0].shape
    nb = others[0].shape[1]
    tiles = width // LANES
    unroll = largest_divisor(tiles, UNROLL)
    flat = [piece.reshape(2 * mb, width) for piece in pieces]
    flat_others = [other.reshape(2 * nb, width) for other in others]
    whole = lambda shape: pl.BlockSpec(shape, lambda i, *_: (0,) * len(shape))
    grid_spec = pltpu.PrefetchScalarGridSpec(
        num_scalar_prefetch=2,
        grid=(tiles // unroll,),
        in_specs=[pl.BlockSpec((2 * mb, unroll * LANES), lambda i, *_: (0, i))] * 4
        + [whole((2 * nb, width))] * len(others)
        + [whole((tiles, LANES)), whole((tiles, LANES))],
        out_specs=[whole((4, 2, mb, nb)), whole((4, 2, nb, mb))],
        scratch_shapes=[pltpu.VMEM((8 * mb, 4 * nb), F32)],
    )
    return pl.pallas_call(
        functools.partial(pair_body, unroll),
        grid_spec=grid_spec,
        out_shape=[
            jax.ShapeDtypeStruct((4, 2, mb, nb), F32),
            jax.ShapeDtypeStruct((4, 2, nb, mb), F32),
        ],
        cost_estimate=pl.CostEstimate(
            flops=160 * mb * nb * width, bytes_accessed=(16 * mb + 4 * nb) * width, transcendentals=0
        ),
    )(tile1, tile2, *flat, *flat_others, rows1, rows2)


def paired(coefficients, shift_map, phase_angle):
    return paired_points(coefficients, shift_map, phase_angle)


def paired_points(coefficients, shift_map, phase_angle):
    raw = coefficients[0]
    k = lax.axis_index("ka")
    j = lax.axis_index("ga")
    points, group = lax.axis_size("ka"), lax.axis_size("ga")
    half = group // 2
    width = shift_map.shape[2]
    tiles = width // LANES
    parity_of = lambda point: (point ^ (point >> 1) ^ (point >> 2)) & 1
    parity = parity_of(k)
    mine = parity * half + j // 2
    theirs = (1 - parity) * half + j // 2
    flips = (4, 2, 1)
    mates = lambda value, mask: lax.ppermute(value, "ga", [(s, s ^ mask) for s in range(group)])
    both = lambda value, pairs: lax.ppermute(value, ("ka", "ga"), pairs)
    middle = [(s, s ^ 6) for s in range(points) if (s >> 1) in (1, 2)]
    outward = [(s, s ^ 2) for s in range(points) if (s >> 1) in (1, 2)]
    hop = lambda value, b: lax.ppermute(value, "ka", [(s, s ^ flips[b]) for s in range(points)])
    along = lambda value, pairs: lax.ppermute(value, "ka", pairs)

    maps = shift_map[0]
    arrived = []
    for value, flip in [(maps, 0)] + [(maps[b : b + 1], flips[b]) for b in range(3)]:
        pairs = [
            ((p ^ flip) * group + parity_of(p) * half + y, p * group + 2 * y)
            for p in range(points)
            for y in range(half)
        ]
        arrived.append(both(value, pairs))
    out_own = block_of(raw, theirs, width)
    arrived = jnp.concatenate(arrived, axis=0)
    swapped_maps = mates(arrived, 1)
    arrived = jnp.where(j % 2 == 0, arrived, swapped_maps) - mine * width

    first1 = hop(out_own, 1)
    parked0 = along(out_own, middle)
    relay_at, out_own = lax.optimization_barrier((theirs ^ 1, out_own))
    out_relay = block_of(raw, relay_at, width)
    relay = mates(out_relay, 2)
    first2 = hop(out_own, 2)
    piece0 = block_of(raw, mine, width)
    piece1 = mates(piece0, 1)
    first0 = [along(first1, middle)]
    first0 += [along(parked0, outward)]
    second1 = hop(relay, 1)
    parked1 = along(relay, middle)
    second2 = hop(relay, 2)
    give = block_of(raw, mine ^ 1, width)
    give, relay = lax.optimization_barrier((give, relay))
    piece2 = mates(give, 2)
    piece3 = mates(piece2, 1)
    pieces = [piece0, piece1, piece2, piece3]
    second0 = [along(second1, middle)]
    second0 += [along(parked1, outward)]
    early = [first0, [first1], [first2]]
    late = [second0, [second1], [second2]]

    tables = []
    place = jnp.arange(tiles, dtype=jnp.int32)
    for b in range(3):
        to_other = arrived[b].reshape(tiles, LANES)
        to_mine = arrived[3 + b].reshape(tiles, LANES)
        tile1 = to_other[:, 0] // LANES
        tile_of = to_mine[:, 0] // LANES
        tile2 = jnp.sum(jnp.where(tile_of[None, :] == place[:, None], place[None, :], 0), axis=1)
        tables.append((tile1, tile2, to_other % LANES, to_mine % LANES))

    sums = [None] * 3
    for b, which in ((2, 0), (2, 1), (1, 0), (1, 1), (0, 0), (0, 1)):
        near, far = pair_products(pieces, (early, late)[which][b], *tables[b])
        mask = 2 * which
        far = both(
            far,
            [
                (p * group + s, (p ^ flips[b]) * group + (s ^ mask))
                for p in range(points)
                for s in range(group)
            ],
        )
        got = [near[0]] + [mates(near[r], r) for r in (1, 2, 3)]
        term = [far[t ^ mask] + got[t ^ mask] for t in range(4)]
        sums[b] = term if sums[b] is None else [x + y for x, y in zip(sums[b], term)]
    stacked = jnp.stack([jnp.stack(one) for one in sums], axis=1)
    ordered = [lax.dynamic_index_in_dim(stacked, j ^ q, 0, keepdims=False) for q in range(4)]
    summed = jnp.concatenate(ordered, axis=-1)
    return rotated_by(phase_angle[0], summed[:, 0], summed[:, 1])[None]


def solution(mesh):
    in_specs = (P("ka", None, "ga", None), P("ka", None, "ga"), P("ka", None))
    out_specs = P("ka", None, None, "ga", None)
    both_ways = mesh.shape["ka"] == 8 and mesh.shape["ga"] == 4
    local = paired if both_ways else general
    return jax.shard_map(local, mesh=mesh, in_specs=in_specs, out_specs=out_specs, check_vma=False)
```
